256 devices in a mesh: seq: 32 (over x, y, core), head: 8 (over z).
Axes of the slice: x: 4, y: 4, z: 8, core: 2. Of those that a mesh axis runs over, the one named last changes fastest.
Arguments:
- tokens: bfloat16 [32768, 2048], P('seq'), may hold values from -6 to 6
- norm_gain: bfloat16 [2048], replicated, may hold values from 0.099609375 to 1.8984375
- w_qkv: bfloat16 [3, 2048, 2048], P(None, None, 'head'), may hold values from -0.176776695 to 0.176776695
- mem_gate: float32 [16], P('head'), may hold values from -3 to 3
- w_out: bfloat16 [2048, 2048], P('head'), may hold values from -0.1875 to 0.1875
Outputs:
- attended: bfloat16 [32768, 2048], P('seq', 'head')
- memory_state: float32 [32, 16, 128, 128], P('seq', 'head')
The draws below stay inside these ranges and needn't reach their ends.
All inputs are finite; a program needn't handle non-finite values.
Results may differ from the reference program's by a relative error of at most 0.01.
The reference program's roundings to bfloat16 on the way count: a program that leaves them out, or rounds other values in their place, can miss the bound.
Values may be sent and summed in bfloat16 or wider, within the bound.
A program may use at most 64 MiB of HBM per device.

```python
import jax
import jax.numpy as jnp
from jax import lax

D = 2048
HEADS = 16
HDIM = 128
SEG = 1024
SEGMENTS = 32
TOKENS = 32768


def draw_w_qkv(key, part):
    base_key = jax.random.fold_in(key, 11)
    drawn = jax.random.truncated_normal(base_key, -6.0, 6.0, (3, D, HEADS * HDIM), jnp.float32) * D ** (-0.5)
    limit_value = 8.0 * D ** (-0.5)
    return jnp.clip(drawn, -limit_value, limit_value).astype(jnp.bfloat16)


def raised(result, own_key, source, target, parts, factor):
    def block_of(position):
        return (jnp.arange(result.shape[position]) // (result.shape[position] // parts)).reshape((-1,) + (1,) * (result.ndim - 1 - position))

    one_side = jax.random.permutation(own_key, parts)[block_of(target)]
    other_side = (block_of(target) + parts // 2) % parts
    return jnp.where((block_of(source) == one_side) | (block_of(source) == other_side), factor * result, result)


def shard_levels(key, dims, shards, smallest, top_value):
    gain, own = 1.0, jax.random.fold_in(key, 6)
    for dim, blocks in shards:
        draws = jnp.exp(jax.random.uniform(jax.random.fold_in(own, dim), (blocks,), jnp.float32, smallest / len(shards), top_value / len(shards)))
        gain = gain * jnp.repeat(draws, dims[dim] // blocks).reshape([-1 if axis == dim else 1 for axis in range(len(dims))])
    return gain


def gaussian(rng, extent, spread, reach, cuts=(), held_as=jnp.bfloat16):
    values = jax.random.normal(rng, extent, jnp.float32) * spread
    if len(cuts) > 0:
        values = shard_levels(rng, extent, cuts, -0.22, 0.18) * values
    return jnp.clip(values, min=-reach, max=reach).astype(held_as)


def gaussian_with(stream_key, dims, width, limit, shards, heavy, dtype=jnp.bfloat16):
    values = width * jax.random.normal(stream_key, dims, jnp.float32)
    if shards:
        values = values * shard_levels(stream_key, dims, shards, -0.22, 0.18)
    return jnp.clip(raised(values, jax.random.fold_in(stream_key, 3), *heavy), -limit, limit).astype(dtype)


def setup_inputs(seed: int = 0) -> dict:
    streams_of = jax.random.split(jax.random.key(seed), 6)
    return {
        "tokens": gaussian(streams_of[0], (TOKENS, D), 1.0, 6.0, ((0, 32),)),
        "norm_gain": jnp.clip(1.0 + 0.18 * jax.random.normal(streams_of[1], (D,), jnp.float32), 0.099609375, 1.8984375).astype(jnp.bfloat16),
        "w_qkv": draw_w_qkv(jax.random.fold_in(streams_of[5], 71), 0),
        "mem_gate": jnp.clip(jax.random.uniform(streams_of[3], (HEADS,), jnp.float32, -3.0, 3.0) * shard_levels(streams_of[3], (HEADS,), ((0, 8),), -0.4, 0.0), -3.0, 3.0),
        "w_out": gaussian_with(streams_of[4], (HEADS * HDIM, D), (HEADS * HDIM) ** -0.5, 0.1875, ((0, 8),), (0, 1, 8, 2.0)),
    }


def elu_one(values_in):
    return jnp.where(values_in > 0, values_in + 1.0, jnp.exp(jnp.minimum(values_in, 0.0)))

def reference(tokens, norm_gain, w_qkv, mem_gate, w_out):
    float_tokens = tokens.astype(jnp.float32)
    normed = (float_tokens * lax.rsqrt(lax.optimization_barrier(jnp.mean(float_tokens * float_tokens, axis=-1, keepdims=True)) + 1e-05) * norm_gain.astype(jnp.float32)).astype(jnp.bfloat16)
    seg_shape = (SEGMENTS, SEG, HEADS, HDIM)
    queries = jnp.dot(normed, w_qkv[0], preferred_element_type=jnp.float32).astype(jnp.bfloat16).reshape(seg_shape)
    key_rows = jnp.dot(normed, w_qkv[1], preferred_element_type=jnp.float32).astype(jnp.bfloat16).reshape(seg_shape)
    value_rows = jnp.dot(normed, w_qkv[2], preferred_element_type=jnp.float32).astype(jnp.bfloat16).reshape(seg_shape)
    sig_keys = elu_one(key_rows.astype(jnp.float32))
    deltas = jnp.einsum('sthd,sthe->shde', sig_keys, value_rows.astype(jnp.float32), precision=lax.Precision.HIGHEST)
    delta_norm = lax.optimization_barrier(jnp.sum(sig_keys, axis=1))
    memory_prev = jnp.concatenate([jnp.zeros_like(deltas[:1]), jnp.cumsum(deltas, axis=0)[:-1]], axis=0)
    norm_prev = jnp.concatenate([jnp.zeros_like(delta_norm[:1]), jnp.cumsum(delta_norm, axis=0)[:-1]], axis=0)
    inv_sqrt = 1.0 / HDIM ** 0.5
    gate_share = jax.nn.sigmoid(mem_gate)[None, :, None]

    def one_segment(segment_parts):
        seg_q, seg_k, seg_v, seg_memory, seg_norm = segment_parts
        scores = jnp.einsum('qhd,khd->hqk', seg_q.astype(jnp.float32), seg_k.astype(jnp.float32)) * inv_sqrt
        row_ids = lax.broadcasted_iota(jnp.int32, (SEG, SEG), 0)
        col_ids = lax.broadcasted_iota(jnp.int32, (SEG, SEG), 1)
        scores = jnp.where((col_ids <= row_ids)[None], scores, -1e+30)
        weights = jax.nn.softmax(scores, axis=-1).astype(jnp.bfloat16)
        local_out = jnp.einsum('hqk,khd->qhd', weights.astype(jnp.float32), seg_v.astype(jnp.float32))
        sig_q = elu_one(seg_q.astype(jnp.float32))
        retrieved = jnp.einsum('thd,hde->the', sig_q, seg_memory, precision=lax.Precision.HIGHEST)
        normalizer = 1.0 + jnp.einsum('thd,hd->th', sig_q, seg_norm, precision=lax.Precision.HIGHEST)
        mixed_out = (gate_share * retrieved / normalizer[..., None] + (1.0 - gate_share) * local_out).astype(jnp.bfloat16)
        return mixed_out.reshape(SEG, HEADS * HDIM)
    mixed_all = lax.map(one_segment, (queries, key_rows, value_rows, memory_prev, norm_prev)).reshape(TOKENS, HEADS * HDIM)
    attended = jnp.dot(mixed_all, w_out, preferred_element_type=jnp.float32).astype(jnp.bfloat16)
    memory_state = (memory_prev + deltas) / SEG
    return (attended, memory_state)
```

```python
import functools

import jax
import jax.numpy as jnp
from jax import lax
from jax.experimental import pallas as pl
from jax.experimental.pallas import tpu as pltpu
from jax.sharding import PartitionSpec as P

HDIM = 128
MESH = pl.DeviceIdType.MESH
F32, BF16 = jnp.float32, jnp.bfloat16
ROWS = 256
LOG2E = 1.4426950408889634


def elu_one(t):
    return jnp.where(t > 0, t + 1.0, jnp.exp(jnp.minimum(t, 0.0)))


def front_kernel(
    tokens, gain, w_qkv, gate, mixed_out, state_out,
    tok, wts, qs, ks, vs, local, own, pay, got_c, got_x, got_y,
    in_sem, send_sem, recv_sem,
):
    seg = tok.shape[0]
    n_chunks = seg // ROWS
    heads = qs.shape[1] // HDIM
    s = lax.axis_index("seq")
    z = lax.axis_index("head")
    x, y, c = s // 8, lax.rem(s // 2, 4), lax.rem(s, 2)

    def at(x2, y2, c2):
        return (x2 * 8 + y2 * 2 + c2, z)

    partner = at(x, y, 1 - c)
    xs = [at(lax.rem(x + k, 4), y, c) for k in (1, 2, 3)]
    ys = [at(x, lax.rem(y + k, 4), c) for k in (1, 2, 3)]

    barrier = pltpu.get_barrier_semaphore()
    for peer in [partner] + xs + ys:
        pl.semaphore_signal(barrier, inc=1, device_id=peer, device_id_type=MESH)

    def load(i, src, dst):
        copy = pltpu.make_async_copy(src, dst, in_sem.at[i])
        copy.start()
        return copy

    rows = [pl.ds(i * ROWS, ROWS) for i in range(n_chunks)]
    tok_copies = [load(0, tokens.at[rows[0]], tok.at[rows[0]])]
    w_copies = [load(n_chunks + j, w_qkv.at[j], wts.at[j]) for j in (1, 2, 0)]
    tok_copies += [load(i, tokens.at[rows[i]], tok.at[rows[i]]) for i in range(1, n_chunks)]

    g = gain[...].astype(F32)
    for i in range(n_chunks):
        tok_copies[i].wait()
        t = tok[rows[i], :].astype(F32)
        scale = lax.rsqrt(jnp.mean(t * t, axis=-1, keepdims=True) + 1e-05)
        normed = (t * scale * g).astype(BF16)
        if i == 0:
            for copy in w_copies:
                copy.wait()
        for j, dst in ((1, ks), (2, vs), (0, qs)):
            dst[rows[i], :] = jnp.dot(normed, wts[j], preferred_element_type=F32).astype(BF16)

    norms = []
    for h in range(heads):
        cols = slice(h * HDIM, (h + 1) * HDIM)
        sig_k = elu_one(ks[:, cols].astype(F32))
        own[cols, :] = lax.dot_general(
            sig_k.astype(BF16), vs[:, cols], (((0,), (0,)), ((), ())), preferred_element_type=F32
        )
        norms.append(jnp.sum(sig_k, axis=0, keepdims=True))
    nrow = lax.broadcasted_iota(jnp.int32, (16, HDIM), 0)
    tail = jnp.zeros((16, HDIM), F32)
    for h in range(heads):
        tail = jnp.where(nrow == h, norms[h], tail)
    own[heads * HDIM :, :] = tail
    pay[0] = own[...].astype(BF16)

    def remote(i, src, dst, peer):
        copy = pltpu.make_async_remote_copy(
            src_ref=src, dst_ref=dst, send_sem=send_sem.at[i], recv_sem=recv_sem.at[i],
            device_id=peer, device_id_type=MESH,
        )
        copy.start()
        return copy

    pl.semaphore_wait(barrier, 7)
    swap = remote(0, pay.at[0], got_c, partner)

    inv_sqrt = LOG2E / HDIM**0.5
    row_ids = lax.broadcasted_iota(jnp.int32, (ROWS, ROWS), 0)
    col_ids = lax.broadcasted_iota(jnp.int32, (ROWS, ROWS), 1)
    causal = col_ids <= row_ids
    shares = jax.nn.sigmoid(gate[...])

    def attend(h, i):
        cols = slice(h * HDIM, (h + 1) * HDIM)
        end = (i + 1) * ROWS
        q = qs[rows[i], cols]
        sc = lax.dot_general(
            q, ks[:end, cols], (((1,), (1,)), ((), ())), preferred_element_type=F32
        )
        diag = jnp.where(causal, sc[:, end - ROWS :], -1e30)
        sc = diag if i == 0 else jnp.concatenate([sc[:, : end - ROWS], diag], axis=1)
        top = jnp.max(sc, axis=-1, keepdims=True)
        e = jnp.exp2((sc - top) * inv_sqrt)
        w = (e * (1.0 / jnp.sum(e, axis=-1, keepdims=True))).astype(BF16)
        out = jnp.dot(w, vs[:end, cols], preferred_element_type=F32)
        local[rows[i], cols] = (1.0 - shares[:, h : h + 1]) * out

    work = [(h, i) for h in range(heads) for i in range(n_chunks)]
    for h, i in work[:1]:
        attend(h, i)
    swap.wait()
    total = own[...] + got_c[...].astype(F32)
    pay[1] = total.astype(BF16)
    x_copies = [remote(k, pay.at[1], got_x.at[k - 1], xs[k - 1]) for k in (1, 2, 3)]
    for h, i in work[1:4]:
        attend(h, i)
    for copy in x_copies:
        copy.wait()
    before = jnp.zeros_like(total)
    for k in (1, 2, 3):
        before += jnp.where(x >= k, got_x[k - 1].astype(F32), 0.0)
    pay[2] = before.astype(BF16)
    pay[3] = (before + total).astype(BF16)
    y_copies = [
        remote(3 + k, pay.at[2 + jnp.where(y + k < 4, 1, 0)], got_y.at[k - 1], ys[k - 1])
        for k in (1, 2, 3)
    ]
    for h, i in work[4:]:
        attend(h, i)
    for copy in y_copies:
        copy.wait()
    prev = before + jnp.where(c == 1, got_c[...].astype(F32), 0.0)
    for k in (1, 2, 3):
        prev += got_y[k - 1].astype(F32)

    for h in range(heads):
        cols = slice(h * HDIM, (h + 1) * HDIM)
        state_out[0, h] = (prev[cols] + own[cols, :]) * (1.0 / seg)
        norm = prev[heads * HDIM + h : heads * HDIM + h + 1]
        norm_cols = jnp.transpose(jnp.broadcast_to(norm, (HDIM, HDIM)))
        memory = jnp.concatenate([prev[cols], norm_cols], axis=1).astype(BF16)
        share = shares[:, h : h + 1]
        for i in range(n_chunks):
            sig_q = elu_one(qs[rows[i], cols].astype(F32)).astype(BF16)
            both = jnp.dot(sig_q, memory, preferred_element_type=F32)
            got = share * both[:, :HDIM] / (1.0 + both[:, HDIM:])
            mixed_out[rows[i], cols] = (got + local[rows[i], cols]).astype(BF16)


def front(tokens, gain, w_qkv, gate):
    seg, d = tokens.shape
    width = w_qkv.shape[2]
    heads = width // HDIM
    n_chunks = seg // ROWS
    pay = (heads * HDIM + 16, HDIM)
    vmem = pl.BlockSpec(memory_space=pltpu.VMEM)
    hbm = pl.BlockSpec(memory_space=pl.ANY)
    return pl.pallas_call(
        front_kernel,
        out_shape=(
            jax.ShapeDtypeStruct((seg, width), BF16),
            jax.ShapeDtypeStruct((1, heads, HDIM, HDIM), F32),
        ),
        in_specs=[hbm, vmem, hbm, vmem],
        out_specs=(vmem, vmem),
        scratch_shapes=[
            pltpu.VMEM((seg, d), BF16),
            pltpu.VMEM((3, d, width), BF16),
            pltpu.VMEM((seg, width), BF16),
            pltpu.VMEM((seg, width), BF16),
            pltpu.VMEM((seg, width), BF16),
            pltpu.VMEM((seg, width), F32),
            pltpu.VMEM(pay, F32),
            pltpu.VMEM((4,) + pay, BF16),
            pltpu.VMEM(pay, BF16),
            pltpu.VMEM((3,) + pay, BF16),
            pltpu.VMEM((3,) + pay, BF16),
            pltpu.SemaphoreType.DMA((n_chunks + 3,)),
            pltpu.SemaphoreType.DMA((7,)),
            pltpu.SemaphoreType.DMA((7,)),
        ],
        compiler_params=pltpu.CompilerParams(
            collective_id=0, has_side_effects=True, vmem_limit_bytes=48 << 20
        ),
        name="front",
    )(tokens, gain, w_qkv, gate)


def on_device(tokens, norm_gain, w_qkv, mem_gate, w_out):
    mixed, state = front(tokens, norm_gain[None], w_qkv, mem_gate[None])
    weight_cols = lax.all_to_all(w_out, "head", split_axis=1, concat_axis=0, tiled=True)
    attended = jnp.dot(
        lax.all_gather(mixed, "head", axis=1, tiled=True),
        weight_cols,
        preferred_element_type=F32,
    ).astype(BF16)
    return attended, state


def solution(mesh):
    placed = (P("seq", None), P(), P(None, None, "head"), P("head"), P("head", None))
    return jax.shard_map(
        on_device,
        mesh=mesh,
        in_specs=placed,
        out_specs=(P("seq", "head"), P("seq", "head", None, None)),
        check_vma=False,
    )
```

```python
import functools

import jax
import jax.numpy as jnp
from jax import lax
from jax.experimental import pallas as pl
from jax.experimental.pallas import tpu as pltpu
from jax.sharding import PartitionSpec as P

HDIM = 128
MESH = pl.DeviceIdType.MESH
F32, BF16 = jnp.float32, jnp.bfloat16
ROWS = 256
LOG2E = 1.4426950408889634


def elu_one(t):
    return jnp.where(t > 0, t + 1.0, jnp.exp(jnp.minimum(t, 0.0)))


def block_kernel(
    tokens, gain, w_qkv, gate, w_out, att_out, state_out,
    tok, wts, qs, ks, vs, local, own, pay, got_c, got_x, got_y,
    mine, mix, wown, wf, outs,
    in_sem, send_sem, recv_sem,
):
    seg = tok.shape[0]
    n_chunks = seg // ROWS
    heads = qs.shape[1] // HDIM
    width = heads * HDIM
    s = lax.axis_index("seq")
    z = lax.axis_index("head")
    x, y, c = s // 8, lax.rem(s // 2, 4), lax.rem(s, 2)
    pair = z // 2
    sign = 2 * lax.rem(z, 2) - 1

    def plane(off):
        return lax.rem(z + sign * off + 8, 8)

    def at(x2, y2, c2):
        return (x2 * 8 + y2 * 2 + c2, z)

    partner = at(x, y, 1 - c)
    xs = [at(lax.rem(x + k, 4), y, c) for k in (1, 2, 3)]
    ys = [at(x, lax.rem(y + k, 4), c) for k in (1, 2, 3)]
    zs = [(s, lax.rem(z + k, 8)) for k in range(1, 8)]
    peers = [partner] + xs + ys + zs

    barrier = pltpu.get_barrier_semaphore()
    for peer in peers:
        pl.semaphore_signal(barrier, inc=1, device_id=peer, device_id_type=MESH)

    def load(i, src, dst):
        copy = pltpu.make_async_copy(src, dst, in_sem.at[i])
        copy.start()
        return copy

    used = [0]

    def remote(src, dst, peer):
        i = used[0]
        used[0] += 1
        copy = pltpu.make_async_remote_copy(
            src_ref=src, dst_ref=dst, send_sem=send_sem.at[i], recv_sem=recv_sem.at[i],
            device_id=peer, device_id_type=MESH,
        )
        copy.start()
        return copy

    def feature_block(owner):
        return pl.ds(pl.multiple_of(owner * width, width), width)

    rows = [pl.ds(i * ROWS, ROWS) for i in range(n_chunks)]
    tok_copies = [load(0, tokens.at[rows[0]], tok.at[rows[0]])]
    w_copies = [load(n_chunks + j, w_qkv.at[j], wts.at[j]) for j in (1, 2, 0)]
    tok_copies += [load(i, tokens.at[rows[i]], tok.at[rows[i]]) for i in range(1, n_chunks)]
    own_copies = [
        load(n_chunks + 3 + k, w_out.at[:, feature_block(plane(k))], wown.at[k]) for k in range(4)
    ]

    g = gain[...].astype(F32).reshape(1, tok.shape[1])

    def project(i):
        tok_copies[i].wait()
        t = tok[rows[i], :].astype(F32)
        scale = lax.rsqrt(jnp.mean(t * t, axis=-1, keepdims=True) + 1e-05)
        normed = (t * scale * g).astype(BF16)
        if i == 0:
            for copy in w_copies:
                copy.wait()
        for j, dst in ((1, ks), (2, vs), (0, qs)):
            dst[rows[i], :] = jnp.dot(normed, wts[j], preferred_element_type=F32).astype(BF16)

    project(0)
    pl.semaphore_wait(barrier, len(peers))
    z_copies = []
    slice_rows = pl.ds(pl.multiple_of((x * 4 + y) * 16, 16), 16)
    for k in range(1, 8):
        there = lax.rem(z + k, 8)
        there_sign = 2 * lax.rem(there, 2) - 1
        for q in range(2):
            owner = lax.rem(there + there_sign * (2 * c + q) + 8, 8)
            z_copies.append(remote(
                w_out.at[slice_rows, feature_block(owner)],
                wf.at[7 - k, 2 * c + q, x, y], zs[k - 1],
            ))
    for i in range(1, n_chunks):
        project(i)

    norms = []
    for h in range(heads):
        cols = slice(h * HDIM, (h + 1) * HDIM)
        sig_k = elu_one(ks[:, cols].astype(F32))
        own[cols, :] = lax.dot_general(
            sig_k.astype(BF16), vs[:, cols], (((0,), (0,)), ((), ())), preferred_element_type=F32
        )
        norms.append(jnp.sum(sig_k, axis=0, keepdims=True))
    nrow = lax.broadcasted_iota(jnp.int32, (16, HDIM), 0)
    tail = jnp.zeros((16, HDIM), F32)
    for h in range(heads):
        tail = jnp.where(nrow == h, norms[h], tail)
    own[heads * HDIM :, :] = tail
    pay[0] = own[...].astype(BF16)
    swap = remote(pay.at[0], got_c, partner)

    inv_sqrt = LOG2E / HDIM**0.5
    row_ids = lax.broadcasted_iota(jnp.int32, (ROWS, ROWS), 0)
    col_ids = lax.broadcasted_iota(jnp.int32, (ROWS, ROWS), 1)
    causal = col_ids <= row_ids
    shares = [jax.nn.sigmoid(jnp.full((1, HDIM), gate[h], F32)) for h in range(heads)]

    def attend(h, i):
        cols = slice(h * HDIM, (h + 1) * HDIM)
        end = (i + 1) * ROWS
        q = qs[rows[i], cols]
        sc = lax.dot_general(
            q, ks[:end, cols], (((1,), (1,)), ((), ())), preferred_element_type=F32
        )
        diag = jnp.where(causal, sc[:, end - ROWS :], -1e30)
        sc = diag if i == 0 else jnp.concatenate([sc[:, : end - ROWS], diag], axis=1)
        top = jnp.max(sc, axis=-1, keepdims=True)
        e = jnp.exp2((sc - top) * inv_sqrt)
        w = (e * (1.0 / jnp.sum(e, axis=-1, keepdims=True))).astype(BF16)
        out = jnp.dot(w, vs[:end, cols], preferred_element_type=F32)
        local[rows[i], cols] = (1.0 - shares[h]) * out

    work = [(h, i) for h in range(heads) for i in range(n_chunks)]
    for copy in z_copies:
        copy.wait()
    one = [remote(wf.at[:, 2 * c, x, y], wf.at[:, 2 * c, x, y], peer) for peer in xs]
    one += [remote(wf.at[:, 2 * c + 1, x, y], wf.at[:, 2 * c + 1, x, y], peer) for peer in ys]
    for h, i in work[:1]:
        attend(h, i)
    swap.wait()
    total = own[...] + got_c[...].astype(F32)
    pay[1] = total.astype(BF16)
    x_copies = [remote(pay.at[1], got_x.at[k - 1], xs[k - 1]) for k in (1, 2, 3)]
    for h, i in work[1:4]:
        attend(h, i)
    for copy in x_copies:
        copy.wait()
    before = jnp.zeros_like(total)
    for k in (1, 2, 3):
        before += jnp.where(x >= k, got_x[k - 1].astype(F32), 0.0)
    pay[2] = before.astype(BF16)
    pay[3] = (before + total).astype(BF16)
    y_copies = [
        remote(pay.at[2 + jnp.where(y + k < 4, 1, 0)], got_y.at[k - 1], ys[k - 1])
        for k in (1, 2, 3)
    ]
    for copy in one:
        copy.wait()
    two = [remote(wf.at[:, 2 * c, :, y], wf.at[:, 2 * c, :, y], peer) for peer in ys]
    two += [remote(wf.at[:, 2 * c + 1, x], wf.at[:, 2 * c + 1, x], peer) for peer in xs]
    for h, i in work[4:]:
        attend(h, i)
    for copy in y_copies:
        copy.wait()
    prev = before + jnp.where(c == 1, got_c[...].astype(F32), 0.0)
    for k in (1, 2, 3):
        prev += got_y[k - 1].astype(F32)

    memories = []
    for h in range(heads):
        cols = slice(h * HDIM, (h + 1) * HDIM)
        state_out[0, h] = (prev[cols] + own[cols, :]) * (1.0 / seg)
        norm = prev[heads * HDIM + h : heads * HDIM + h + 1]
        norm_cols = jnp.transpose(jnp.broadcast_to(norm, (HDIM, HDIM)))
        memories.append(jnp.concatenate([prev[cols], norm_cols], axis=1).astype(BF16))

    def blend(slot, quarter):
        block = pl.ds(pl.multiple_of(quarter * ROWS, ROWS), ROWS)
        for h in range(heads):
            cols = slice(h * HDIM, (h + 1) * HDIM)
            sig_q = elu_one(qs[block, cols].astype(F32)).astype(BF16)
            both = jnp.dot(sig_q, memories[h], preferred_element_type=F32)
            got = shares[h] * both[:, :HDIM] / (1.0 + both[:, HDIM:])
            mine[slot, :, cols] = (got + local[block, cols]).astype(BF16)

    towards = {1: plane(1), 2: plane(-2), 3: plane(3)}
    straight = {}
    for k in (3, 2, 1):
        blend(k, towards[k] // 2)
        straight[k] = remote(mine.at[k], mix.at[k - 1], (s, towards[k]))
    blend(0, pair)
    beside = (s, plane(-1))
    next_door = remote(mine.at[0], mix.at[3], beside)
    handed = {}
    for k in (1, 2, 3):
        straight[k].wait()
        handed[k] = remote(mix.at[k - 1], mix.at[3 + k], beside)
    for copy in two:
        copy.wait()
    both_cores = remote(wf.at[:, pl.ds(2 * c, 2)], wf.at[:, pl.ds(2 * c, 2)], partner)
    for copy in own_copies:
        copy.wait()
    next_door.wait()
    both_cores.wait()

    def place(off):
        return lax.rem(sign * off + 8, 8) - 1

    def weight(off, k):
        return wf[place(off), k].reshape(width, width)

    sums = []
    for k in range(4):
        acc = jnp.dot(mine[0], wown[k], preferred_element_type=F32)
        for slot, off in ((0, 1), (1, 2), (2, 3), (3, -1)):
            acc += jnp.dot(mix[slot], weight(off, k), preferred_element_type=F32)
        sums.append(acc)
    for k in (1, 2, 3):
        handed[k].wait()
    here = pl.ds(pl.multiple_of(pair * ROWS, ROWS), ROWS)
    last = []
    for k in (3, 2, 1, 0):
        acc = sums[k]
        for slot, off in ((4, -2), (5, -3), (6, -4)):
            acc += jnp.dot(mix[slot], weight(off, k), preferred_element_type=F32)
        if k == 0:
            att_out[here, :] = acc.astype(BF16)
        else:
            outs[k - 1] = acc.astype(BF16)
            last.append(remote(outs.at[k - 1], att_out.at[here], (s, plane(k))))
    for copy in last:
        copy.wait()


def block(tokens, gain, w_qkv, gate, w_out):
    seg, d = tokens.shape
    width = w_qkv.shape[2]
    heads = width // HDIM
    n_chunks = seg // ROWS
    pay = (heads * HDIM + 16, HDIM)
    vmem = pl.BlockSpec(memory_space=pltpu.VMEM)
    hbm = pl.BlockSpec(memory_space=pl.ANY)
    return pl.pallas_call(
        block_kernel,
        out_shape=(
            jax.ShapeDtypeStruct((seg, width), BF16),
            jax.ShapeDtypeStruct((1, heads, HDIM, HDIM), F32),
        ),
        in_specs=[hbm, vmem, hbm, pl.BlockSpec(memory_space=pltpu.SMEM), hbm],
        out_specs=(vmem, vmem),
        scratch_shapes=[
            pltpu.VMEM((seg, d), BF16),
            pltpu.VMEM((3, d, width), BF16),
            pltpu.VMEM((seg, width), BF16),
            pltpu.VMEM((seg, width), BF16),
            pltpu.VMEM((seg, width), BF16),
            pltpu.VMEM((seg, width), F32),
            pltpu.VMEM(pay, F32),
            pltpu.VMEM((4,) + pay, BF16),
            pltpu.VMEM(pay, BF16),
            pltpu.VMEM((3,) + pay, BF16),
            pltpu.VMEM((3,) + pay, BF16),
            pltpu.VMEM((4, ROWS, width), BF16),
            pltpu.VMEM((7, ROWS, width), BF16),
            pltpu.VMEM((4, width, width), BF16),
            pltpu.VMEM((7, 4, 4, 4, 16, width), BF16),
            pltpu.VMEM((3, ROWS, width), BF16),
            pltpu.SemaphoreType.DMA((n_chunks + 7,)),
            pltpu.SemaphoreType.DMA((48,)),
            pltpu.SemaphoreType.DMA((48,)),
        ],
        compiler_params=pltpu.CompilerParams(
            collective_id=0, has_side_effects=True, vmem_limit_bytes=60 << 20
        ),
        name="block",
    )(tokens, gain, w_qkv, gate, w_out)


def settle_kernel(att, state, att_out, state_out):
    att_out[...] = att[...]
    state_out[...] = state[...]


def settle(*arrays):
    vmem = pl.BlockSpec(memory_space=pltpu.VMEM)
    return pl.pallas_call(
        settle_kernel,
        out_shape=tuple(jax.ShapeDtypeStruct(a.shape, a.dtype) for a in arrays),
        in_specs=[vmem, vmem],
        out_specs=(vmem, vmem),
        compiler_params=pltpu.CompilerParams(vmem_limit_bytes=60 << 20),
        name="settle",
    )(*arrays)


def on_device(tokens, norm_gain, w_qkv, mem_gate, w_out):
    return settle(*block(tokens, norm_gain, w_qkv, mem_gate, w_out))


def solution(mesh):
    placed = (P("seq", None), P(), P(None, None, "head"), P("head"), P("head", None))
    return jax.shard_map(
        on_device,
        mesh=mesh,
        in_specs=placed,
        out_specs=(P("seq", "head"), P("seq", "head", None, None)),
        check_vma=False,
    )
```

```python
import functools

import jax
import jax.numpy as jnp
from jax import lax
from jax.experimental import pallas as pl
from jax.experimental.pallas import tpu as pltpu
from jax.sharding import PartitionSpec as P

HDIM = 128
MESH = pl.DeviceIdType.MESH
F32, BF16 = jnp.float32, jnp.bfloat16
ROWS = 256
LOG2E = 1.4426950408889634


def elu_one(t):
    return jnp.where(t > 0, t + 1.0, jnp.exp(jnp.minimum(t, 0.0)))


def block_kernel(
    tokens, gain, w_qkv, gate, w_out, att_out, state_out,
    tok, wts, qs, ks, vs, local, own, pay, got_c, got_x, got_y,
    mine, mix, wown, wf, outs,
    in_sem, send_sem, recv_sem,
):
    seg = tok.shape[0]
    n_chunks = seg // ROWS
    heads = qs.shape[1] // HDIM
    width = heads * HDIM
    s = lax.axis_index("seq")
    z = lax.axis_index("head")
    x, y, c = s // 8, lax.rem(s // 2, 4), lax.rem(s, 2)
    pair = z // 2
    sign = 2 * lax.rem(z, 2) - 1

    def plane(off):
        return lax.rem(z + sign * off + 8, 8)

    def at(x2, y2, c2):
        return (x2 * 8 + y2 * 2 + c2, z)

    partner = at(x, y, 1 - c)
    xs = [at(lax.rem(x + k, 4), y, c) for k in (1, 2, 3)]
    ys = [at(x, lax.rem(y + k, 4), c) for k in (1, 2, 3)]
    zs = [(s, lax.rem(z + k, 8)) for k in range(1, 8)]
    peers = [partner] + xs + ys + zs

    barrier = pltpu.get_barrier_semaphore()
    for peer in peers:
        pl.semaphore_signal(barrier, inc=1, device_id=peer, device_id_type=MESH)

    def load(i, src, dst):
        copy = pltpu.make_async_copy(src, dst, in_sem.at[i])
        copy.start()
        return copy

    used = [0]

    def remote(src, dst, peer):
        i = used[0]
        used[0] += 1
        copy = pltpu.make_async_remote_copy(
            src_ref=src, dst_ref=dst, send_sem=send_sem.at[i], recv_sem=recv_sem.at[i],
            device_id=peer, device_id_type=MESH,
        )
        copy.start()
        return copy

    def feature_block(owner):
        return pl.ds(pl.multiple_of(owner * width, width), width)

    rows = [pl.ds(i * ROWS, ROWS) for i in range(n_chunks)]
    tok_copies = [load(0, tokens.at[rows[0]], tok.at[rows[0]])]
    w_copies = [load(n_chunks + j, w_qkv.at[j], wts.at[j]) for j in (1, 2, 0)]
    tok_copies += [load(i, tokens.at[rows[i]], tok.at[rows[i]]) for i in range(1, n_chunks)]
    own_copies = [
        load(n_chunks + 3 + k, w_out.at[:, feature_block(plane(k))], wown.at[k]) for k in range(4)
    ]

    g = gain[...].astype(F32).reshape(1, tok.shape[1])

    def normalize(i):
        tok_copies[i].wait()
        t = tok[rows[i], :].astype(F32)
        scale = lax.rsqrt(jnp.mean(t * t, axis=-1, keepdims=True) + 1e-05)
        tok[rows[i], :] = (t * scale * g).astype(BF16)

    def project(i, j, dst):
        out = jnp.dot(tok[rows[i], :], wts[j], preferred_element_type=F32)
        dst[rows[i], :] = out.astype(BF16)

    normalize(0)
    w_copies[0].wait()
    w_copies[1].wait()
    for i in range(n_chunks):
        if i + 1 < n_chunks:
            normalize(i + 1)
        project(i, 1, ks)
        project(i, 2, vs)
        if i == 0:
            pl.semaphore_wait(barrier, len(peers))
            z_copies = []
            slice_rows = pl.ds(pl.multiple_of((x * 4 + y) * 16, 16), 16)
            for k in range(1, 8):
                there = lax.rem(z + k, 8)
                there_sign = 2 * lax.rem(there, 2) - 1
                for q in range(2):
                    owner = lax.rem(there + there_sign * (2 * c + q) + 8, 8)
                    z_copies.append(remote(
                        w_out.at[slice_rows, feature_block(owner)],
                        wf.at[7 - k, 2 * c + q, x, y], zs[k - 1],
                    ))

    norms = []
    for h in range(heads):
        cols = slice(h * HDIM, (h + 1) * HDIM)
        sig_k = elu_one(ks[:, cols].astype(F32))
        own[cols, :] = lax.dot_general(
            sig_k.astype(BF16), vs[:, cols], (((0,), (0,)), ((), ())), preferred_element_type=F32
        )
        norms.append(jnp.sum(sig_k, axis=0, keepdims=True))
    nrow = lax.broadcasted_iota(jnp.int32, (16, HDIM), 0)
    tail = jnp.zeros((16, HDIM), F32)
    for h in range(heads):
        tail = jnp.where(nrow == h, norms[h], tail)
    own[heads * HDIM :, :] = tail
    pay[0] = own[...].astype(BF16)
    swap = remote(pay.at[0], got_c, partner)

    inv_sqrt = LOG2E / HDIM**0.5
    row_ids = lax.broadcasted_iota(jnp.int32, (ROWS, ROWS), 0)
    col_ids = lax.broadcasted_iota(jnp.int32, (ROWS, ROWS), 1)
    causal = col_ids <= row_ids
    shares = [jax.nn.sigmoid(jnp.full((1, HDIM), gate[h], F32)) for h in range(heads)]

    def attend(h, i):
        cols = slice(h * HDIM, (h + 1) * HDIM)
        end = (i + 1) * ROWS
        q = qs[rows[i], cols]
        sc = lax.dot_general(
            q, ks[:end, cols], (((1,), (1,)), ((), ())), preferred_element_type=F32
        )
        diag = jnp.where(causal, sc[:, end - ROWS :], -1e30)
        sc = diag if i == 0 else jnp.concatenate([sc[:, : end - ROWS], diag], axis=1)
        top = jnp.max(sc, axis=-1, keepdims=True)
        e = jnp.exp2((sc - top) * inv_sqrt)
        w = (e * (1.0 / jnp.sum(e, axis=-1, keepdims=True))).astype(BF16)
        out = jnp.dot(w, vs[:end, cols], preferred_element_type=F32)
        local[rows[i], cols] = (1.0 - shares[h]) * out

    work = [(h, i) for h in range(heads) for i in range(n_chunks)]
    w_copies[2].wait()
    for i in range(n_chunks):
        project(i, 0, qs)
    for copy in z_copies:
        copy.wait()
    one = [remote(wf.at[:, 2 * c, x, y], wf.at[:, 2 * c, x, y], peer) for peer in xs]
    one += [remote(wf.at[:, 2 * c + 1, x, y], wf.at[:, 2 * c + 1, x, y], peer) for peer in ys]
    swap.wait()
    total = own[...] + got_c[...].astype(F32)
    pay[1] = total.astype(BF16)
    x_copies = [remote(pay.at[1], got_x.at[k - 1], xs[k - 1]) for k in (1, 2, 3)]
    for h, i in work[:4]:
        attend(h, i)
    for copy in x_copies:
        copy.wait()
    before = jnp.zeros_like(total)
    for k in (1, 2, 3):
        before += jnp.where(x >= k, got_x[k - 1].astype(F32), 0.0)
    pay[2] = before.astype(BF16)
    pay[3] = (before + total).astype(BF16)
    y_copies = [
        remote(pay.at[2 + jnp.where(y + k < 4, 1, 0)], got_y.at[k - 1], ys[k - 1])
        for k in (1, 2, 3)
    ]
    for copy in one:
        copy.wait()
    two = [remote(wf.at[:, 2 * c, :, y], wf.at[:, 2 * c, :, y], peer) for peer in ys]
    two += [remote(wf.at[:, 2 * c + 1, x], wf.at[:, 2 * c + 1, x], peer) for peer in xs]
    across = [
        remote(wf.at[:, 2 * c, :, y], wf.at[:, 2 * c, :, y], partner),
        remote(wf.at[:, 2 * c + 1, x], wf.at[:, 2 * c + 1, x], partner),
    ]
    for h, i in work[4:]:
        attend(h, i)
    for i in range(n_chunks):
        qs[rows[i], :] = elu_one(qs[rows[i], :].astype(F32)).astype(BF16)
    for copy in y_copies:
        copy.wait()
    prev = before + jnp.where(c == 1, got_c[...].astype(F32), 0.0)
    for k in (1, 2, 3):
        prev += got_y[k - 1].astype(F32)

    memories = []
    for h in range(heads):
        cols = slice(h * HDIM, (h + 1) * HDIM)
        state_out[0, h] = (prev[cols] + own[cols, :]) * (1.0 / seg)
        norm = prev[heads * HDIM + h : heads * HDIM + h + 1]
        norm_cols = jnp.transpose(jnp.broadcast_to(norm, (HDIM, HDIM)))
        memories.append(jnp.concatenate([prev[cols], norm_cols], axis=1).astype(BF16))

    half = ROWS // 2

    def blend(slot, quarter, t):
        block = pl.ds(pl.multiple_of(quarter * ROWS + t * half, half), half)
        for h in range(heads):
            cols = slice(h * HDIM, (h + 1) * HDIM)
            both = jnp.dot(qs[block, cols], memories[h], preferred_element_type=F32)
            got = shares[h] * both[:, :HDIM] / (1.0 + both[:, HDIM:])
            mine[slot, t, :, cols] = (got + local[block, cols]).astype(BF16)

    towards = {1: plane(1), 2: plane(-2), 3: plane(3)}
    beside = (s, plane(-1))
    straight, next_door, handed = {}, {}, {}
    for t in range(2):
        for k in (3, 2, 1):
            blend(k, towards[k] // 2, t)
            straight[t, k] = remote(mine.at[k, t], mix.at[k - 1, t], (s, towards[k]))
        blend(0, pair, t)
        next_door[t] = remote(mine.at[0, t], mix.at[3, t], beside)
    for t in range(2):
        for k in (1, 2, 3):
            straight[t, k].wait()
            handed[t, k] = remote(mix.at[k - 1, t], mix.at[3 + k, t], beside)
        if t == 0:
            for k in (1, 2, 3):
                two[k - 1].wait()
                spot = wf.at[:, 2 * c, :, lax.rem(y + 4 - k, 4)]
                across.append(remote(spot, spot, partner))
                two[k + 2].wait()
                spot = wf.at[:, 2 * c + 1, lax.rem(x + 4 - k, 4)]
                across.append(remote(spot, spot, partner))
    for copy in own_copies:
        copy.wait()
    for copy in across:
        copy.wait()

    def place(off):
        return lax.rem(sign * off + 8, 8) - 1

    def weight(off, k):
        return wf[place(off), k].reshape(width, width)

    last = []
    for t in range(2):
        next_door[t].wait()
        sums = []
        for k in range(4):
            acc = jnp.dot(mine[0, t], wown[k], preferred_element_type=F32)
            for slot, off in ((0, 1), (1, 2), (2, 3), (3, -1)):
                acc += jnp.dot(mix[slot, t], weight(off, k), preferred_element_type=F32)
            sums.append(acc)
        for k in (1, 2, 3):
            handed[t, k].wait()
        here = pl.ds(pl.multiple_of(pair * ROWS + t * half, half), half)
        for k in (3, 2, 1, 0):
            acc = sums[k]
            for slot, off in ((4, -2), (5, -3), (6, -4)):
                acc += jnp.dot(mix[slot, t], weight(off, k), preferred_element_type=F32)
            if k == 0:
                att_out[here, :] = acc.astype(BF16)
            else:
                outs[k - 1, t] = acc.astype(BF16)
                last.append(remote(outs.at[k - 1, t], att_out.at[here], (s, plane(k))))
    for copy in last:
        copy.wait()


def block(tokens, gain, w_qkv, gate, w_out):
    seg, d = tokens.shape
    width = w_qkv.shape[2]
    heads = width // HDIM
    n_chunks = seg // ROWS
    pay = (heads * HDIM + 16, HDIM)
    vmem = pl.BlockSpec(memory_space=pltpu.VMEM)
    hbm = pl.BlockSpec(memory_space=pl.ANY)
    return pl.pallas_call(
        block_kernel,
        out_shape=(
            jax.ShapeDtypeStruct((seg, width), BF16),
            jax.ShapeDtypeStruct((1, heads, HDIM, HDIM), F32),
        ),
        in_specs=[hbm, vmem, hbm, pl.BlockSpec(memory_space=pltpu.SMEM), hbm],
        out_specs=(vmem, vmem),
        scratch_shapes=[
            pltpu.VMEM((seg, d), BF16),
            pltpu.VMEM((3, d, width), BF16),
            pltpu.VMEM((seg, width), BF16),
            pltpu.VMEM((seg, width), BF16),
            pltpu.VMEM((seg, width), BF16),
            pltpu.VMEM((seg, width), F32),
            pltpu.VMEM(pay, F32),
            pltpu.VMEM((4,) + pay, BF16),
            pltpu.VMEM(pay, BF16),
            pltpu.VMEM((3,) + pay, BF16),
            pltpu.VMEM((3,) + pay, BF16),
            pltpu.VMEM((4, 2, ROWS // 2, width), BF16),
            pltpu.VMEM((7, 2, ROWS // 2, width), BF16),
            pltpu.VMEM((4, width, width), BF16),
            pltpu.VMEM((7, 4, 4, 4, 16, width), BF16),
            pltpu.VMEM((3, 2, ROWS // 2, width), BF16),
            pltpu.SemaphoreType.DMA((n_chunks + 7,)),
            pltpu.SemaphoreType.DMA((64,)),
            pltpu.SemaphoreType.DMA((64,)),
        ],
        compiler_params=pltpu.CompilerParams(
            collective_id=0, has_side_effects=True, vmem_limit_bytes=60 << 20
        ),
        name="block",
    )(tokens, gain, w_qkv, gate, w_out)


def settle_kernel(att, state, att_out, state_out):
    att_out[...] = att[...]
    state_out[...] = state[...]


def settle(*arrays):
    vmem = pl.BlockSpec(memory_space=pltpu.VMEM)
    return pl.pallas_call(
        settle_kernel,
        out_shape=tuple(jax.ShapeDtypeStruct(a.shape, a.dtype) for a in arrays),
        in_specs=[vmem, vmem],
        out_specs=(vmem, vmem),
        compiler_params=pltpu.CompilerParams(vmem_limit_bytes=60 << 20),
        name="settle",
    )(*arrays)


def on_device(tokens, norm_gain, w_qkv, mem_gate, w_out):
    return settle(*block(tokens, norm_gain, w_qkv, mem_gate, w_out))


def solution(mesh):
    placed = (P("seq", None), P(), P(None, None, "head"), P("head"), P("head", None))
    return jax.shard_map(
        on_device,
        mesh=mesh,
        in_specs=placed,
        out_specs=(P("seq", "head"), P("seq", "head", None, None)),
        check_vma=False,
    )
```

```python
import functools

import jax
import jax.numpy as jnp
from jax import lax
from jax.experimental import pallas as pl
from jax.experimental.pallas import tpu as pltpu
from jax.sharding import PartitionSpec as P

HDIM = 128
MESH = pl.DeviceIdType.MESH
F32, BF16 = jnp.float32, jnp.bfloat16
ROWS = 256
LOG2E = 1.4426950408889634


def elu_one(t):
    return jnp.where(t > 0, t + 1.0, jnp.exp(jnp.minimum(t, 0.0)))


def block_kernel(
    tokens, gain, w_qkv, gate, w_out, att_out, state_out,
    tok, wkv, wq, qs, ks, vs, local, own, pay, got_c, got_x, got_y,
    mine, mix, wown, wf, outs,
    in_sem, send_sem, recv_sem,
):
    seg = tok.shape[0]
    n_chunks = seg // ROWS
    heads = qs.shape[1] // HDIM
    width = heads * HDIM
    s = lax.axis_index("seq")
    z = lax.axis_index("head")
    x, y, c = s // 8, lax.rem(s // 2, 4), lax.rem(s, 2)
    pair = z // 2
    sign = 2 * lax.rem(z, 2) - 1

    def plane(off):
        return lax.rem(z + sign * off + 8, 8)

    def at(x2, y2, c2):
        return (x2 * 8 + y2 * 2 + c2, z)

    partner = at(x, y, 1 - c)
    xs = [at(lax.rem(x + k, 4), y, c) for k in (1, 2, 3)]
    ys = [at(x, lax.rem(y + k, 4), c) for k in (1, 2, 3)]
    zs = [(s, lax.rem(z + k, 8)) for k in range(1, 8)]
    peers = [partner] + xs + ys + zs

    barrier = pltpu.get_barrier_semaphore()
    for peer in peers:
        pl.semaphore_signal(barrier, inc=1, device_id=peer, device_id_type=MESH)

    def load(i, src, dst):
        copy = pltpu.make_async_copy(src, dst, in_sem.at[i])
        copy.start()
        return copy

    used = [0]

    def remote(src, dst, peer):
        i = used[0]
        used[0] += 1
        copy = pltpu.make_async_remote_copy(
            src_ref=src, dst_ref=dst, send_sem=send_sem.at[i], recv_sem=recv_sem.at[i],
            device_id=peer, device_id_type=MESH,
        )
        copy.start()
        return copy

    def feature_block(owner):
        return pl.ds(pl.multiple_of(owner * width, width), width)

    rows = [pl.ds(i * ROWS, ROWS) for i in range(n_chunks)]
    head_cols = [slice(h * HDIM, (h + 1) * HDIM) for h in range(heads)]

    def load_tokens(i):
        return load(i, tokens.at[rows[i]], tok.at[rows[i]])

    def load_pair(h):
        return [
            load(n_chunks + 2 * h + j, w_qkv.at[1 + j, :, head_cols[h]], wkv.at[h, :, head_cols[j]])
            for j in range(2)
        ]

    tok_copies = [load_tokens(0)]
    pairs = [load_pair(0)]
    tok_copies.append(load_tokens(1))

    g = gain[...].astype(F32).reshape(1, tok.shape[1])

    def normalize(i):
        tok_copies[i].wait()
        if i + 2 < n_chunks:
            tok_copies.append(load_tokens(i + 2))
        t = tok[rows[i], :].astype(F32)
        scale = lax.rsqrt(jnp.mean(t * t, axis=-1, keepdims=True) + 1e-05)
        tok[rows[i], :] = (t * scale * g).astype(BF16)

    def project_pair(i, h):
        out = jnp.dot(tok[rows[i], :], wkv[h], preferred_element_type=F32).astype(BF16)
        ks[rows[i], head_cols[h]] = out[:, :HDIM]
        vs[rows[i], head_cols[h]] = out[:, HDIM:]

    def find_delta(h):
        sig_k = elu_one(ks[:, head_cols[h]].astype(F32))
        own[h, :HDIM] = lax.dot_general(
            sig_k.astype(BF16), vs[:, head_cols[h]], (((0,), (0,)), ((), ())),
            preferred_element_type=F32,
        )
        own[h, HDIM:] = jnp.broadcast_to(jnp.sum(sig_k, axis=0, keepdims=True), (16, HDIM))
        pay[h, 0] = own[h].astype(BF16)
        return remote(pay.at[h, 0], got_c.at[h], partner)

    normalize(0)
    for copy in pairs[0]:
        copy.wait()
    for i in range(n_chunks):
        if i + 1 < n_chunks:
            normalize(i + 1)
        if i == 2:
            pairs.append(load_pair(1))
            q_copy = load(n_chunks + 4, w_qkv.at[0], wq)
            own_copies = [
                load(n_chunks + 5 + k, w_out.at[:, feature_block(plane(k))], wown.at[k])
                for k in range(4)
            ]
        project_pair(i, 0)
        if i == 0:
            pl.semaphore_wait(barrier, len(peers))
            z_copies = []
            slice_rows = pl.ds(pl.multiple_of((x * 4 + y) * 16, 16), 16)
            for k in range(1, 8):
                there = lax.rem(z + k, 8)
                there_sign = 2 * lax.rem(there, 2) - 1
                for q in range(2):
                    owner = lax.rem(there + there_sign * (2 * c + q) + 8, 8)
                    z_copies.append(remote(
                        w_out.at[slice_rows, feature_block(owner)],
                        wf.at[7 - k, 2 * c + q, x, y], zs[k - 1],
                    ))
    swaps = [find_delta(0)]
    for copy in pairs[1]:
        copy.wait()
    for i in range(n_chunks):
        project_pair(i, 1)

    totals, befores, x_copies, y_copies = {}, {}, {}, {}

    def send_x(h):
        swaps[h].wait()
        totals[h] = own[h] + got_c[h].astype(F32)
        pay[h, 1] = totals[h].astype(BF16)
        x_copies[h] = [remote(pay.at[h, 1], got_x.at[h, k - 1], xs[k - 1]) for k in (1, 2, 3)]

    def send_y(h):
        for copy in x_copies[h]:
            copy.wait()
        before = jnp.zeros_like(totals[h])
        for k in (1, 2, 3):
            before += jnp.where(x >= k, got_x[h, k - 1].astype(F32), 0.0)
        befores[h] = before
        pay[h, 2] = before.astype(BF16)
        pay[h, 3] = (before + totals[h]).astype(BF16)
        y_copies[h] = [
            remote(pay.at[h, 2 + jnp.where(y + k < 4, 1, 0)], got_y.at[h, k - 1], ys[k - 1])
            for k in (1, 2, 3)
        ]

    def finish_prefix(h):
        for copy in y_copies[h]:
            copy.wait()
        prev = befores[h] + jnp.where(c == 1, got_c[h].astype(F32), 0.0)
        for k in (1, 2, 3):
            prev += got_y[h, k - 1].astype(F32)
        state_out[0, h] = (prev[:HDIM] + own[h, :HDIM]) * (1.0 / seg)
        norm_cols = jnp.transpose(jnp.broadcast_to(prev[HDIM : HDIM + 1], (HDIM, HDIM)))
        return jnp.concatenate([prev[:HDIM], norm_cols], axis=1).astype(BF16)

    inv_sqrt = LOG2E / HDIM**0.5
    row_ids = lax.broadcasted_iota(jnp.int32, (ROWS, ROWS), 0)
    col_ids = lax.broadcasted_iota(jnp.int32, (ROWS, ROWS), 1)
    causal = col_ids <= row_ids
    shares = [jax.nn.sigmoid(jnp.full((1, HDIM), gate[h], F32)) for h in range(heads)]

    def attend(h, i):
        cols = slice(h * HDIM, (h + 1) * HDIM)
        end = (i + 1) * ROWS
        q = qs[rows[i], cols]
        sc = lax.dot_general(
            q, ks[:end, cols], (((1,), (1,)), ((), ())), preferred_element_type=F32
        )
        diag = jnp.where(causal, sc[:, end - ROWS :], -1e30)
        sc = diag if i == 0 else jnp.concatenate([sc[:, : end - ROWS], diag], axis=1)
        top = jnp.max(sc, axis=-1, keepdims=True)
        e = jnp.exp2((sc - top) * inv_sqrt)
        w = (e * (1.0 / jnp.sum(e, axis=-1, keepdims=True))).astype(BF16)
        out = jnp.dot(w, vs[:end, cols], preferred_element_type=F32)
        local[rows[i], cols] = (1.0 - shares[h]) * out

    swaps.append(find_delta(1))
    send_x(0)
    q_copy.wait()
    for i in range(n_chunks):
        qs[rows[i], :] = jnp.dot(tok[rows[i], :], wq[...], preferred_element_type=F32).astype(BF16)
    send_x(1)
    for copy in z_copies:
        copy.wait()
    one = [remote(wf.at[:, 2 * c, x, y], wf.at[:, 2 * c, x, y], peer) for peer in xs]
    one += [remote(wf.at[:, 2 * c + 1, x, y], wf.at[:, 2 * c + 1, x, y], peer) for peer in ys]
    for i in range(n_chunks):
        attend(0, i)
    send_y(0)
    send_y(1)
    for i in range(n_chunks - 1):
        attend(1, i)
    for copy in one:
        copy.wait()
    two = [remote(wf.at[:, 2 * c, :, y], wf.at[:, 2 * c, :, y], peer) for peer in ys]
    two += [remote(wf.at[:, 2 * c + 1, x], wf.at[:, 2 * c + 1, x], peer) for peer in xs]
    across = [
        remote(wf.at[:, 2 * c, :, y], wf.at[:, 2 * c, :, y], partner),
        remote(wf.at[:, 2 * c + 1, x], wf.at[:, 2 * c + 1, x], partner),
    ]
    attend(1, n_chunks - 1)
    for i in range(n_chunks):
        qs[rows[i], :] = elu_one(qs[rows[i], :].astype(F32)).astype(BF16)
    memories = {}

    half = ROWS // 2

    def blend(slot, quarter, t, h):
        block = pl.ds(pl.multiple_of(quarter * ROWS + t * half, half), half)
        both = jnp.dot(qs[block, head_cols[h]], memories[h], preferred_element_type=F32)
        got = shares[h] * both[:, :HDIM] / (1.0 + both[:, HDIM:])
        mine[slot, t, h] = (got + local[block, head_cols[h]]).astype(BF16)

    towards = {1: plane(1), 2: plane(-2), 3: plane(3)}
    beside = (s, plane(-1))
    straight, next_door, handed = {}, {}, {}
    for t in range(2):
        for h in range(heads):
            if t == 0:
                memories[h] = finish_prefix(h)
            for k in (3, 2, 1):
                blend(k, towards[k] // 2, t, h)
                straight[t, k, h] = remote(
                    mine.at[k, t, h], mix.at[k - 1, t, h], (s, towards[k])
                )
            blend(0, pair, t, h)
            next_door[t, h] = remote(mine.at[0, t, h], mix.at[3, t, h], beside)
    for t in range(2):
        for k in (1, 2, 3):
            for h in range(heads):
                straight[t, k, h].wait()
            handed[t, k] = remote(mix.at[k - 1, t], mix.at[3 + k, t], beside)
        if t == 0:
            for k in (1, 2, 3):
                two[k - 1].wait()
                spot = wf.at[:, 2 * c, :, lax.rem(y + 4 - k, 4)]
                across.append(remote(spot, spot, partner))
                two[k + 2].wait()
                spot = wf.at[:, 2 * c + 1, lax.rem(x + 4 - k, 4)]
                across.append(remote(spot, spot, partner))
    for copy in own_copies:
        copy.wait()
    for copy in across:
        copy.wait()

    def place(off):
        return lax.rem(sign * off + 8, 8) - 1

    def gathered(buffer, *at_slot):
        return jnp.concatenate([buffer[(*at_slot, h)] for h in range(heads)], axis=1)

    def weight(off, k):
        return wf[place(off), k].reshape(width, width)

    last = []
    for t in range(2):
        for h in range(heads):
            next_door[t, h].wait()
        sums = []
        for k in range(4):
            acc = jnp.dot(gathered(mine, 0, t), wown[k], preferred_element_type=F32)
            for slot, off in ((0, 1), (1, 2), (2, 3), (3, -1)):
                acc += jnp.dot(gathered(mix, slot, t), weight(off, k), preferred_element_type=F32)
            sums.append(acc)
        for k in (1, 2, 3):
            handed[t, k].wait()
        here = pl.ds(pl.multiple_of(pair * ROWS + t * half, half), half)
        for k in (3, 2, 1, 0):
            acc = sums[k]
            for slot, off in ((4, -2), (5, -3), (6, -4)):
                acc += jnp.dot(gathered(mix, slot, t), weight(off, k), preferred_element_type=F32)
            if k == 0:
                att_out[here, :] = acc.astype(BF16)
            else:
                outs[k - 1, t] = acc.astype(BF16)
                last.append(remote(outs.at[k - 1, t], att_out.at[here], (s, plane(k))))
    for copy in last:
        copy.wait()


def block(tokens, gain, w_qkv, gate, w_out):
    seg, d = tokens.shape
    width = w_qkv.shape[2]
    heads = width // HDIM
    n_chunks = seg // ROWS
    pay = (HDIM + 16, HDIM)
    vmem = pl.BlockSpec(memory_space=pltpu.VMEM)
    hbm = pl.BlockSpec(memory_space=pl.ANY)
    return pl.pallas_call(
        block_kernel,
        out_shape=(
            jax.ShapeDtypeStruct((seg, width), BF16),
            jax.ShapeDtypeStruct((1, heads, HDIM, HDIM), F32),
        ),
        in_specs=[hbm, vmem, hbm, pl.BlockSpec(memory_space=pltpu.SMEM), hbm],
        out_specs=(vmem, vmem),
        scratch_shapes=[
            pltpu.VMEM((seg, d), BF16),
            pltpu.VMEM((heads, d, 2 * HDIM), BF16),
            pltpu.VMEM((d, width), BF16),
            pltpu.VMEM((seg, width), BF16),
            pltpu.VMEM((seg, width), BF16),
            pltpu.VMEM((seg, width), BF16),
            pltpu.VMEM((seg, width), F32),
            pltpu.VMEM((heads,) + pay, F32),
            pltpu.VMEM((heads, 4) + pay, BF16),
            pltpu.VMEM((heads,) + pay, BF16),
            pltpu.VMEM((heads, 3) + pay, BF16),
            pltpu.VMEM((heads, 3) + pay, BF16),
            pltpu.VMEM((4, 2, heads, ROWS // 2, HDIM), BF16),
            pltpu.VMEM((7, 2, heads, ROWS // 2, HDIM), BF16),
            pltpu.VMEM((4, width, width), BF16),
            pltpu.VMEM((7, 4, 4, 4, 16, width), BF16),
            pltpu.VMEM((3, 2, ROWS // 2, width), BF16),
            pltpu.SemaphoreType.DMA((n_chunks + 9,)),
            pltpu.SemaphoreType.DMA((80,)),
            pltpu.SemaphoreType.DMA((80,)),
        ],
        compiler_params=pltpu.CompilerParams(
            collective_id=0, has_side_effects=True, vmem_limit_bytes=60 << 20
        ),
        name="block",
    )(tokens, gain, w_qkv, gate, w_out)


def settle_kernel(att, state, att_out, state_out):
    att_out[...] = att[...]
    state_out[...] = state[...]


def settle(*arrays):
    vmem = pl.BlockSpec(memory_space=pltpu.VMEM)
    return pl.pallas_call(
        settle_kernel,
        out_shape=tuple(jax.ShapeDtypeStruct(a.shape, a.dtype) for a in arrays),
        in_specs=[vmem, vmem],
        out_specs=(vmem, vmem),
        compiler_params=pltpu.CompilerParams(vmem_limit_bytes=60 << 20),
        name="settle",
    )(*arrays)


def on_device(tokens, norm_gain, w_qkv, mem_gate, w_out):
    return settle(*block(tokens, norm_gain, w_qkv, mem_gate, w_out))


def solution(mesh):
    placed = (P("seq", None), P(), P(None, None, "head"), P("head"), P("head", None))
    return jax.shard_map(
        on_device,
        mesh=mesh,
        in_specs=placed,
        out_specs=(P("seq", "head"), P("seq", "head", None, None)),
        check_vma=False,
    )
```

```python
import functools

import jax
import jax.numpy as jnp
from jax import lax
from jax.experimental import pallas as pl
from jax.experimental.pallas import tpu as pltpu
from jax.sharding import PartitionSpec as P

HDIM = 128
MESH = pl.DeviceIdType.MESH
F32, BF16 = jnp.float32, jnp.bfloat16
ROWS = 256
LOG2E = 1.4426950408889634


def elu_one(t):
    return jnp.where(t > 0, t + 1.0, jnp.exp(jnp.minimum(t, 0.0)))


def block_kernel(
    tokens, gain_in, w_qkv, gate_in, w_out, att_out, state_out,
    gain, gate, tok, wkv, wq, qs, ks, vs, local, own, pay, got_c, got_x, got_y,
    mine, mix, wown, wf, outs,
    in_sem, send_sem, recv_sem,
):
    seg = tok.shape[0]
    n_chunks = seg // ROWS
    heads = qs.shape[1] // HDIM
    width = heads * HDIM
    s = lax.axis_index("seq")
    z = lax.axis_index("head")
    x, y, c = s // 8, lax.rem(s // 2, 4), lax.rem(s, 2)
    pair = z // 2
    sign = 2 * lax.rem(z, 2) - 1

    def plane(off):
        return lax.rem(z + sign * off + 8, 8)

    def at(x2, y2, c2):
        return (x2 * 8 + y2 * 2 + c2, z)

    partner = at(x, y, 1 - c)
    xs = [at(lax.rem(x + k, 4), y, c) for k in (1, 2, 3)]
    ys = [at(x, lax.rem(y + k, 4), c) for k in (1, 2, 3)]
    zs = [(s, lax.rem(z + k, 8)) for k in range(1, 8)]
    peers = [partner] + xs + ys + zs

    barrier = pltpu.get_barrier_semaphore()
    for peer in peers:
        pl.semaphore_signal(barrier, inc=1, device_id=peer, device_id_type=MESH)

    def load(i, src, dst):
        copy = pltpu.make_async_copy(src, dst, in_sem.at[i])
        copy.start()
        return copy

    used = [0]

    def remote(src, dst, peer):
        i = used[0]
        used[0] += 1
        copy = pltpu.make_async_remote_copy(
            src_ref=src, dst_ref=dst, send_sem=send_sem.at[i], recv_sem=recv_sem.at[i],
            device_id=peer, device_id_type=MESH,
        )
        copy.start()
        return copy

    def feature_block(owner):
        return pl.ds(pl.multiple_of(owner * width, width), width)

    rows = [pl.ds(i * ROWS, ROWS) for i in range(n_chunks)]
    head_cols = [slice(h * HDIM, (h + 1) * HDIM) for h in range(heads)]

    def load_tokens(i):
        return load(i, tokens.at[rows[i]], tok.at[rows[i]])

    def load_pair(h):
        return [
            load(n_chunks + 2 * h + j, w_qkv.at[1 + j, :, head_cols[h]], wkv.at[h, :, head_cols[j]])
            for j in range(2)
        ]

    gain_copy = load(n_chunks + 9, gain_in, gain)
    gate_copy = load(n_chunks + 10, gate_in, gate)
    tok_copies = [load_tokens(0)]
    pairs = [load_pair(0)]
    tok_copies.append(load_tokens(1))

    gain_copy.wait()
    gate_copy.wait()
    g = gain[...].astype(F32).reshape(1, tok.shape[1])

    def normalize(i):
        tok_copies[i].wait()
        if i + 2 < n_chunks:
            tok_copies.append(load_tokens(i + 2))
        t = tok[rows[i], :].astype(F32)
        scale = lax.rsqrt(jnp.mean(t * t, axis=-1, keepdims=True) + 1e-05)
        tok[rows[i], :] = (t * scale * g).astype(BF16)

    def project_pair(i, h):
        out = jnp.dot(tok[rows[i], :], wkv[h], preferred_element_type=F32).astype(BF16)
        ks[rows[i], head_cols[h]] = out[:, :HDIM]
        vs[rows[i], head_cols[h]] = out[:, HDIM:]

    def find_delta(h):
        sig_k = elu_one(ks[:, head_cols[h]].astype(F32))
        own[h, :HDIM] = lax.dot_general(
            sig_k.astype(BF16), vs[:, head_cols[h]], (((0,), (0,)), ((), ())),
            preferred_element_type=F32,
        )
        own[h, HDIM:] = jnp.broadcast_to(jnp.sum(sig_k, axis=0, keepdims=True), (16, HDIM))
        pay[h, 0] = own[h].astype(BF16)
        return remote(pay.at[h, 0], got_c.at[h], partner)

    normalize(0)
    for copy in pairs[0]:
        copy.wait()
    for i in range(n_chunks):
        if i + 1 < n_chunks:
            normalize(i + 1)
        if i == 2:
            pairs.append(load_pair(1))
            q_copy = load(n_chunks + 4, w_qkv.at[0], wq)
            own_copies = [
                load(n_chunks + 5 + k, w_out.at[:, feature_block(plane(k))], wown.at[k])
                for k in range(4)
            ]
        project_pair(i, 0)
        if i == 0:
            pl.semaphore_wait(barrier, len(peers))
            z_copies = []
            slice_rows = pl.ds(pl.multiple_of((x * 4 + y) * 16, 16), 16)
            for k in range(1, 8):
                there = lax.rem(z + k, 8)
                there_sign = 2 * lax.rem(there, 2) - 1
                for q in range(2):
                    owner = lax.rem(there + there_sign * (2 * c + q) + 8, 8)
                    z_copies.append(remote(
                        w_out.at[slice_rows, feature_block(owner)],
                        wf.at[7 - k, 2 * c + q, x, y], zs[k - 1],
                    ))
    swaps = [find_delta(0)]
    for copy in pairs[1]:
        copy.wait()
    for i in range(n_chunks):
        project_pair(i, 1)

    totals, befores, x_copies, y_copies = {}, {}, {}, {}

    def send_x(h):
        swaps[h].wait()
        totals[h] = own[h] + got_c[h].astype(F32)
        pay[h, 1] = totals[h].astype(BF16)
        x_copies[h] = [remote(pay.at[h, 1], got_x.at[h, k - 1], xs[k - 1]) for k in (1, 2, 3)]

    def send_y(h):
        for copy in x_copies[h]:
            copy.wait()
        before = jnp.zeros_like(totals[h])
        for k in (1, 2, 3):
            before += jnp.where(x >= k, got_x[h, k - 1].astype(F32), 0.0)
        befores[h] = before
        pay[h, 2] = before.astype(BF16)
        pay[h, 3] = (before + totals[h]).astype(BF16)
        y_copies[h] = [
            remote(pay.at[h, 2 + jnp.where(y + k < 4, 1, 0)], got_y.at[h, k - 1], ys[k - 1])
            for k in (1, 2, 3)
        ]

    def finish_prefix(h):
        for copy in y_copies[h]:
            copy.wait()
        prev = befores[h] + jnp.where(c == 1, got_c[h].astype(F32), 0.0)
        for k in (1, 2, 3):
            prev += got_y[h, k - 1].astype(F32)
        state_out[0, h] = (prev[:HDIM] + own[h, :HDIM]) * (1.0 / seg)
        norm_cols = jnp.transpose(jnp.broadcast_to(prev[HDIM : HDIM + 1], (HDIM, HDIM)))
        return jnp.concatenate([prev[:HDIM], norm_cols], axis=1).astype(BF16)

    inv_sqrt = LOG2E / HDIM**0.5
    row_ids = lax.broadcasted_iota(jnp.int32, (ROWS, ROWS), 0)
    col_ids = lax.broadcasted_iota(jnp.int32, (ROWS, ROWS), 1)
    causal = col_ids <= row_ids
    shares = [jax.nn.sigmoid(jnp.full((1, HDIM), gate[h], F32)) for h in range(heads)]

    def attend(h, i):
        cols = slice(h * HDIM, (h + 1) * HDIM)
        end = (i + 1) * ROWS
        q = qs[rows[i], cols]
        sc = lax.dot_general(
            q, ks[:end, cols], (((1,), (1,)), ((), ())), preferred_element_type=F32
        )
        diag = jnp.where(causal, sc[:, end - ROWS :], -1e30)
        sc = diag if i == 0 else jnp.concatenate([sc[:, : end - ROWS], diag], axis=1)
        top = jnp.max(sc, axis=-1, keepdims=True)
        e = jnp.exp2((sc - top) * inv_sqrt)
        w = (e * (1.0 / jnp.sum(e, axis=-1, keepdims=True))).astype(BF16)
        out = jnp.dot(w, vs[:end, cols], preferred_element_type=F32)
        local[rows[i], cols] = (1.0 - shares[h]) * out

    swaps.append(find_delta(1))
    send_x(0)
    q_copy.wait()
    for i in range(n_chunks):
        qs[rows[i], :] = jnp.dot(tok[rows[i], :], wq[...], preferred_element_type=F32).astype(BF16)
    send_x(1)
    for copy in z_copies:
        copy.wait()
    one = [remote(wf.at[:, 2 * c, x, y], wf.at[:, 2 * c, x, y], peer) for peer in xs]
    one += [remote(wf.at[:, 2 * c + 1, x, y], wf.at[:, 2 * c + 1, x, y], peer) for peer in ys]
    for i in range(n_chunks):
        attend(0, i)
    send_y(0)
    send_y(1)
    for i in range(n_chunks - 1):
        attend(1, i)
    for copy in one:
        copy.wait()
    two = [remote(wf.at[:, 2 * c, :, y], wf.at[:, 2 * c, :, y], peer) for peer in ys]
    two += [remote(wf.at[:, 2 * c + 1, x], wf.at[:, 2 * c + 1, x], peer) for peer in xs]
    across = [
        remote(wf.at[:, 2 * c, :, y], wf.at[:, 2 * c, :, y], partner),
        remote(wf.at[:, 2 * c + 1, x], wf.at[:, 2 * c + 1, x], partner),
    ]
    attend(1, n_chunks - 1)
    for i in range(n_chunks):
        qs[rows[i], :] = elu_one(qs[rows[i], :].astype(F32)).astype(BF16)
    memories = {}

    half = ROWS // 2

    def blend(slot, quarter, t, h):
        block = pl.ds(pl.multiple_of(quarter * ROWS + t * half, half), half)
        both = jnp.dot(qs[block, head_cols[h]], memories[h], preferred_element_type=F32)
        got = shares[h] * both[:, :HDIM] / (1.0 + both[:, HDIM:])
        mine[slot, t, h] = (got + local[block, head_cols[h]]).astype(BF16)

    towards = {1: plane(1), 2: plane(-2), 3: plane(3)}
    beside = (s, plane(-1))
    straight, next_door, handed = {}, {}, {}
    for t in range(2):
        for h in range(heads):
            if t == 0:
                memories[h] = finish_prefix(h)
            for k in (3, 2, 1):
                blend(k, towards[k] // 2, t, h)
                straight[t, k, h] = remote(
                    mine.at[k, t, h], mix.at[k - 1, t, h], (s, towards[k])
                )
            blend(0, pair, t, h)
            next_door[t, h] = remote(mine.at[0, t, h], mix.at[3, t, h], beside)
    for t in range(2):
        for k in (1, 2, 3):
            for h in range(heads):
                straight[t, k, h].wait()
            handed[t, k] = remote(mix.at[k - 1, t], mix.at[3 + k, t], beside)
        if t == 0:
            for k in (1, 2, 3):
                two[k - 1].wait()
                spot = wf.at[:, 2 * c, :, lax.rem(y + 4 - k, 4)]
                across.append(remote(spot, spot, partner))
                two[k + 2].wait()
                spot = wf.at[:, 2 * c + 1, lax.rem(x + 4 - k, 4)]
                across.append(remote(spot, spot, partner))
    for copy in own_copies:
        copy.wait()
    for copy in across:
        copy.wait()

    def place(off):
        return lax.rem(sign * off + 8, 8) - 1

    def gathered(buffer, *at_slot):
        return jnp.concatenate([buffer[(*at_slot, h)] for h in range(heads)], axis=1)

    def weight(off, k):
        return wf[place(off), k].reshape(width, width)

    last = []
    for t in range(2):
        for h in range(heads):
            next_door[t, h].wait()
        sums = []
        for k in range(4):
            acc = jnp.dot(gathered(mine, 0, t), wown[k], preferred_element_type=F32)
            for slot, off in ((0, 1), (1, 2), (2, 3), (3, -1)):
                acc += jnp.dot(gathered(mix, slot, t), weight(off, k), preferred_element_type=F32)
            sums.append(acc)
        for k in (1, 2, 3):
            handed[t, k].wait()
        here = pl.ds(pl.multiple_of(pair * ROWS + t * half, half), half)
        for k in (3, 2, 1, 0):
            acc = sums[k]
            for slot, off in ((4, -2), (5, -3), (6, -4)):
                acc += jnp.dot(gathered(mix, slot, t), weight(off, k), preferred_element_type=F32)
            if k == 0:
                att_out[here, :] = acc.astype(BF16)
            else:
                outs[k - 1, t] = acc.astype(BF16)
                last.append(remote(outs.at[k - 1, t], att_out.at[here], (s, plane(k))))
    for copy in last:
        copy.wait()


def block(tokens, gain, w_qkv, gate, w_out):
    seg, d = tokens.shape
    width = w_qkv.shape[2]
    heads = width // HDIM
    n_chunks = seg // ROWS
    pay = (HDIM + 16, HDIM)
    vmem = pl.BlockSpec(memory_space=pltpu.VMEM)
    hbm = pl.BlockSpec(memory_space=pl.ANY)
    return pl.pallas_call(
        block_kernel,
        out_shape=(
            jax.ShapeDtypeStruct((seg, width), BF16),
            jax.ShapeDtypeStruct((1, heads, HDIM, HDIM), F32),
        ),
        in_specs=[hbm] * 5,
        out_specs=(vmem, vmem),
        scratch_shapes=[
            pltpu.VMEM((d,), BF16),
            pltpu.SMEM((heads,), F32),
            pltpu.VMEM((seg, d), BF16),
            pltpu.VMEM((heads, d, 2 * HDIM), BF16),
            pltpu.VMEM((d, width), BF16),
            pltpu.VMEM((seg, width), BF16),
            pltpu.VMEM((seg, width), BF16),
            pltpu.VMEM((seg, width), BF16),
            pltpu.VMEM((seg, width), F32),
            pltpu.VMEM((heads,) + pay, F32),
            pltpu.VMEM((heads, 4) + pay, BF16),
            pltpu.VMEM((heads,) + pay, BF16),
            pltpu.VMEM((heads, 3) + pay, BF16),
            pltpu.VMEM((heads, 3) + pay, BF16),
            pltpu.VMEM((4, 2, heads, ROWS // 2, HDIM), BF16),
            pltpu.VMEM((7, 2, heads, ROWS // 2, HDIM), BF16),
            pltpu.VMEM((4, width, width), BF16),
            pltpu.VMEM((7, 4, 4, 4, 16, width), BF16),
            pltpu.VMEM((3, 2, ROWS // 2, width), BF16),
            pltpu.SemaphoreType.DMA((n_chunks + 11,)),
            pltpu.SemaphoreType.DMA((80,)),
            pltpu.SemaphoreType.DMA((80,)),
        ],
        compiler_params=pltpu.CompilerParams(
            collective_id=0, has_side_effects=True, vmem_limit_bytes=53 << 20
        ),
        name="block",
    )(tokens, gain, w_qkv, gate, w_out)


def settle_kernel(att, state, att_out, state_out):
    att_out[...] = att[...]
    state_out[...] = state[...]


def settle(*arrays):
    vmem = pl.BlockSpec(memory_space=pltpu.VMEM)
    return pl.pallas_call(
        settle_kernel,
        out_shape=tuple(jax.ShapeDtypeStruct(a.shape, a.dtype) for a in arrays),
        in_specs=[vmem, vmem],
        out_specs=(vmem, vmem),
        compiler_params=pltpu.CompilerParams(vmem_limit_bytes=8 << 20),
        name="settle",
    )(*arrays)


def on_device(tokens, norm_gain, w_qkv, mem_gate, w_out):
    norm_gain = pltpu.with_memory_space_constraint(norm_gain, pltpu.HBM)
    mem_gate = pltpu.with_memory_space_constraint(mem_gate, pltpu.HBM)
    return settle(*block(tokens, norm_gain, w_qkv, mem_gate, w_out))


def solution(mesh):
    placed = (P("seq", None), P(), P(None, None, "head"), P("head"), P("head", None))
    return jax.shard_map(
        on_device,
        mesh=mesh,
        in_specs=placed,
        out_specs=(P("seq", "head"), P("seq", "head", None, None)),
        check_vma=False,
    )
```

```python
import functools

import jax
import jax.numpy as jnp
from jax import lax
from jax.experimental import pallas as pl
from jax.experimental.pallas import tpu as pltpu
from jax.sharding import PartitionSpec as P

HDIM = 128
MESH = pl.DeviceIdType.MESH
F32, BF16 = jnp.float32, jnp.bfloat16
ROWS = 256
LOG2E = 1.4426950408889634


def elu_one(t):
    return jnp.where(t > 0, t + 1.0, jnp.exp(jnp.minimum(t, 0.0)))


def block_kernel(
    tokens, gain_in, w_qkv, gate_in, w_out, att_out, state_out,
    gain, gate, tok, wkv, wq, qs, ks, vs, local, own, pay, got_c, got_x, got_y,
    mine, mix, wown, wf, outs,
    in_sem, send_sem, recv_sem,
):
    seg = tok.shape[0]
    n_chunks = seg // ROWS
    heads = qs.shape[1] // HDIM
    width = heads * HDIM
    s = lax.axis_index("seq")
    z = lax.axis_index("head")
    x, y, c = s // 8, lax.rem(s // 2, 4), lax.rem(s, 2)
    pair = z // 2
    sign = 2 * lax.rem(z, 2) - 1

    def plane(off):
        return lax.rem(z + sign * off + 8, 8)

    def at(x2, y2, c2):
        return (x2 * 8 + y2 * 2 + c2, z)

    partner = at(x, y, 1 - c)
    xs = [at(lax.rem(x + k, 4), y, c) for k in (1, 2, 3)]
    ys = [at(x, lax.rem(y + k, 4), c) for k in (1, 2, 3)]
    zs = [(s, lax.rem(z + k, 8)) for k in range(1, 8)]
    peers = [partner] + xs + ys + zs

    got_x[...] = jnp.zeros_like(got_x)
    barrier = pltpu.get_barrier_semaphore()
    for peer in peers:
        pl.semaphore_signal(barrier, inc=1, device_id=peer, device_id_type=MESH)

    def load(i, src, dst):
        copy = pltpu.make_async_copy(src, dst, in_sem.at[i])
        copy.start()
        return copy

    used = [0]

    def remote(src, dst, peer, wanted=None):
        i = used[0]
        used[0] += 1
        copy = pltpu.make_async_remote_copy(
            src_ref=src, dst_ref=dst, send_sem=send_sem.at[i], recv_sem=recv_sem.at[i],
            device_id=peer, device_id_type=MESH,
        )
        if wanted is None:
            copy.start()
        else:
            pl.when(wanted)(copy.start)
        return copy

    def feature_block(owner):
        return pl.ds(pl.multiple_of(owner * width, width), width)

    rows = [pl.ds(i * ROWS, ROWS) for i in range(n_chunks)]
    head_cols = [slice(h * HDIM, (h + 1) * HDIM) for h in range(heads)]

    def load_tokens(i):
        return load(i, tokens.at[rows[i]], tok.at[rows[i]])

    def load_pair(h):
        return [
            load(n_chunks + 2 * h + j, w_qkv.at[1 + j, :, head_cols[h]], wkv.at[h, :, head_cols[j]])
            for j in range(2)
        ]

    gain_copy = load(n_chunks + 9, gain_in, gain)
    gate_copy = load(n_chunks + 10, gate_in, gate)
    tok_copies = [load_tokens(0)]
    pairs = [load_pair(0)]
    tok_copies.append(load_tokens(1))

    gain_copy.wait()
    gate_copy.wait()
    g = gain[...].astype(F32).reshape(1, tok.shape[1])

    def normalize(i):
        tok_copies[i].wait()
        if i + 2 < n_chunks:
            tok_copies.append(load_tokens(i + 2))
        t = tok[rows[i], :].astype(F32)
        scale = lax.rsqrt(jnp.mean(t * t, axis=-1, keepdims=True) + 1e-05)
        tok[rows[i], :] = (t * scale * g).astype(BF16)

    def project_pair(i, h):
        out = jnp.dot(tok[rows[i], :], wkv[h], preferred_element_type=F32).astype(BF16)
        ks[rows[i], head_cols[h]] = out[:, :HDIM]
        vs[rows[i], head_cols[h]] = out[:, HDIM:]

    def find_delta(h):
        sig_k = elu_one(ks[:, head_cols[h]].astype(F32))
        own[h, :HDIM] = lax.dot_general(
            sig_k.astype(BF16), vs[:, head_cols[h]], (((0,), (0,)), ((), ())),
            preferred_element_type=F32,
        )
        own[h, HDIM:] = jnp.broadcast_to(jnp.sum(sig_k, axis=0, keepdims=True), (16, HDIM))
        pay[h, 0] = own[h].astype(BF16)
        return remote(pay.at[h, 0], got_c.at[h], partner)

    normalize(0)
    for copy in pairs[0]:
        copy.wait()
    for i in range(n_chunks):
        if i + 1 < n_chunks:
            normalize(i + 1)
        if i == 2:
            pairs.append(load_pair(1))
            q_copy = load(n_chunks + 4, w_qkv.at[0], wq)
            own_copies = [
                load(n_chunks + 5 + k, w_out.at[:, feature_block(plane(k))], wown.at[k])
                for k in range(4)
            ]
        project_pair(i, 0)
        if i == 0:
            pl.semaphore_wait(barrier, len(peers))
            z_copies = []
            slice_rows = pl.ds(pl.multiple_of((x * 4 + y) * 16, 16), 16)
            for k in range(1, 8):
                there = lax.rem(z + k, 8)
                there_sign = 2 * lax.rem(there, 2) - 1
                for q in range(2):
                    owner = lax.rem(there + there_sign * (2 * c + q) + 8, 8)
                    z_copies.append(remote(
                        w_out.at[slice_rows, feature_block(owner)],
                        wf.at[7 - k, 2 * c + q, x, y], zs[k - 1],
                    ))
    swaps = [find_delta(0)]
    for copy in pairs[1]:
        copy.wait()
    for i in range(n_chunks):
        project_pair(i, 1)

    totals, befores, x_copies, y_copies = {}, {}, {}, {}

    def send_x(h):
        swaps[h].wait()
        totals[h] = own[h] + got_c[h].astype(F32)
        pay[h, 1] = totals[h].astype(BF16)
        x_copies[h] = [
            remote(pay.at[h, 1], got_x.at[h, k - 1], xs[k - 1], x + k < 4) for k in (1, 2, 3)
        ]

    def send_y(h):
        for k in (1, 2, 3):
            pl.when(x + k < 4)(x_copies[h][k - 1].wait_send)
            pl.when(x >= k)(x_copies[h][k - 1].wait_recv)
        before = jnp.zeros_like(totals[h])
        for k in (1, 2, 3):
            before += jnp.where(x >= k, got_x[h, k - 1].astype(F32), 0.0)
        befores[h] = before
        pay[h, 2] = before.astype(BF16)
        pay[h, 3] = (before + totals[h]).astype(BF16)
        y_copies[h] = [
            remote(pay.at[h, 2 + jnp.where(y + k < 4, 1, 0)], got_y.at[h, k - 1], ys[k - 1])
            for k in (1, 2, 3)
        ]

    def finish_prefix(h):
        for copy in y_copies[h]:
            copy.wait()
        prev = befores[h] + jnp.where(c == 1, got_c[h].astype(F32), 0.0)
        for k in (1, 2, 3):
            prev += got_y[h, k - 1].astype(F32)
        state_out[0, h] = (prev[:HDIM] + own[h, :HDIM]) * (1.0 / seg)
        norm_cols = jnp.transpose(jnp.broadcast_to(prev[HDIM : HDIM + 1], (HDIM, HDIM)))
        return jnp.concatenate([prev[:HDIM], norm_cols], axis=1).astype(BF16)

    inv_sqrt = LOG2E / HDIM**0.5
    row_ids = lax.broadcasted_iota(jnp.int32, (ROWS, ROWS), 0)
    col_ids = lax.broadcasted_iota(jnp.int32, (ROWS, ROWS), 1)
    causal = col_ids <= row_ids
    shares = [jax.nn.sigmoid(jnp.full((1, HDIM), gate[h], F32)) for h in range(heads)]

    def attend(h, i):
        cols = slice(h * HDIM, (h + 1) * HDIM)
        end = (i + 1) * ROWS
        q = qs[rows[i], cols]
        sc = lax.dot_general(
            q, ks[:end, cols], (((1,), (1,)), ((), ())), preferred_element_type=F32
        )
        diag = jnp.where(causal, sc[:, end - ROWS :], -1e30)
        sc = diag if i == 0 else jnp.concatenate([sc[:, : end - ROWS], diag], axis=1)
        top = jnp.max(sc, axis=-1, keepdims=True)
        e = jnp.exp2((sc - top) * inv_sqrt)
        w = (e * (1.0 / jnp.sum(e, axis=-1, keepdims=True))).astype(BF16)
        out = jnp.dot(w, vs[:end, cols], preferred_element_type=F32)
        local[rows[i], cols] = (1.0 - shares[h]) * out

    swaps.append(find_delta(1))
    send_x(0)
    q_copy.wait()
    for i in range(n_chunks):
        qs[rows[i], :] = jnp.dot(tok[rows[i], :], wq[...], preferred_element_type=F32).astype(BF16)
    send_x(1)
    for copy in z_copies:
        copy.wait()
    one = [remote(wf.at[:, 2 * c, x, y], wf.at[:, 2 * c, x, y], peer) for peer in xs]
    one += [remote(wf.at[:, 2 * c + 1, x, y], wf.at[:, 2 * c + 1, x, y], peer) for peer in ys]
    for i in range(n_chunks):
        attend(0, i)
    send_y(0)
    for i in range(n_chunks - 2):
        attend(1, i)
    send_y(1)
    attend(1, n_chunks - 2)
    for copy in one:
        copy.wait()
    two = [remote(wf.at[:, 2 * c, :, y], wf.at[:, 2 * c, :, y], peer) for peer in ys]
    two += [remote(wf.at[:, 2 * c + 1, x], wf.at[:, 2 * c + 1, x], peer) for peer in xs]
    across = [
        remote(wf.at[:, 2 * c, :, y], wf.at[:, 2 * c, :, y], partner),
        remote(wf.at[:, 2 * c + 1, x], wf.at[:, 2 * c + 1, x], partner),
    ]
    attend(1, n_chunks - 1)
    for i in range(n_chunks):
        qs[rows[i], :] = elu_one(qs[rows[i], :].astype(F32)).astype(BF16)
    memories = {}

    half = ROWS // 2

    def blend(slot, quarter, t, h):
        block = pl.ds(pl.multiple_of(quarter * ROWS + t * half, half), half)
        both = jnp.dot(qs[block, head_cols[h]], memories[h], preferred_element_type=F32)
        got = shares[h] * both[:, :HDIM] / (1.0 + both[:, HDIM:])
        mine[slot, t, h] = (got + local[block, head_cols[h]]).astype(BF16)

    towards = {1: plane(1), 2: plane(-2), 3: plane(3)}
    beside = (s, plane(-1))
    straight, next_door, handed = {}, {}, {}
    for t in range(2):
        for h in range(heads):
            if t == 0:
                memories[h] = finish_prefix(h)
            for k in (3, 2, 1):
                blend(k, towards[k] // 2, t, h)
                straight[t, k, h] = remote(
                    mine.at[k, t, h], mix.at[k - 1, t, h], (s, towards[k])
                )
            blend(0, pair, t, h)
            next_door[t, h] = remote(mine.at[0, t, h], mix.at[3, t, h], beside)
    for t in range(2):
        for k in (1, 2, 3):
            for h in range(heads):
                straight[t, k, h].wait()
            handed[t, k] = remote(mix.at[k - 1, t], mix.at[3 + k, t], beside)
        if t == 0:
            for k in (1, 2, 3):
                two[k - 1].wait()
                spot = wf.at[:, 2 * c, :, lax.rem(y + 4 - k, 4)]
                across.append(remote(spot, spot, partner))
                two[k + 2].wait()
                spot = wf.at[:, 2 * c + 1, lax.rem(x + 4 - k, 4)]
                across.append(remote(spot, spot, partner))
    for copy in own_copies:
        copy.wait()
    for copy in across:
        copy.wait()

    def place(off):
        return lax.rem(sign * off + 8, 8) - 1

    def gathered(buffer, *at_slot):
        return jnp.concatenate([buffer[(*at_slot, h)] for h in range(heads)], axis=1)

    def weight(off, k):
        return wf[place(off), k].reshape(width, width)

    last = []
    for t in range(2):
        for h in range(heads):
            next_door[t, h].wait()
        sums = []
        for k in range(4):
            acc = jnp.dot(gathered(mine, 0, t), wown[k], preferred_element_type=F32)
            for slot, off in ((0, 1), (1, 2), (2, 3), (3, -1)):
                acc += jnp.dot(gathered(mix, slot, t), weight(off, k), preferred_element_type=F32)
            sums.append(acc)
        for k in (1, 2, 3):
            handed[t, k].wait()
        here = pl.ds(pl.multiple_of(pair * ROWS + t * half, half), half)
        for k in (3, 2, 1, 0):
            acc = sums[k]
            for slot, off in ((4, -2), (5, -3), (6, -4)):
                acc += jnp.dot(gathered(mix, slot, t), weight(off, k), preferred_element_type=F32)
            if k == 0:
                att_out[here, :] = acc.astype(BF16)
            else:
                outs[k - 1, t] = acc.astype(BF16)
                last.append(remote(outs.at[k - 1, t], att_out.at[here], (s, plane(k))))
    for copy in last:
        copy.wait()


def block(tokens, gain, w_qkv, gate, w_out):
    seg, d = tokens.shape
    width = w_qkv.shape[2]
    heads = width // HDIM
    n_chunks = seg // ROWS
    pay = (HDIM + 16, HDIM)
    vmem = pl.BlockSpec(memory_space=pltpu.VMEM)
    hbm = pl.BlockSpec(memory_space=pl.ANY)
    return pl.pallas_call(
        block_kernel,
        out_shape=(
            jax.ShapeDtypeStruct((seg, width), BF16),
            jax.ShapeDtypeStruct((1, heads, HDIM, HDIM), F32),
        ),
        in_specs=[hbm] * 5,
        out_specs=(vmem, vmem),
        scratch_shapes=[
            pltpu.VMEM((d,), BF16),
            pltpu.SMEM((heads,), F32),
            pltpu.VMEM((seg, d), BF16),
            pltpu.VMEM((heads, d, 2 * HDIM), BF16),
            pltpu.VMEM((d, width), BF16),
            pltpu.VMEM((seg, width), BF16),
            pltpu.VMEM((seg, width), BF16),
            pltpu.VMEM((seg, width), BF16),
            pltpu.VMEM((seg, width), F32),
            pltpu.VMEM((heads,) + pay, F32),
            pltpu.VMEM((heads, 4) + pay, BF16),
            pltpu.VMEM((heads,) + pay, BF16),
            pltpu.VMEM((heads, 3) + pay, BF16),
            pltpu.VMEM((heads, 3) + pay, BF16),
            pltpu.VMEM((4, 2, heads, ROWS // 2, HDIM), BF16),
            pltpu.VMEM((7, 2, heads, ROWS // 2, HDIM), BF16),
            pltpu.VMEM((4, width, width), BF16),
            pltpu.VMEM((7, 4, 4, 4, 16, width), BF16),
            pltpu.VMEM((3, 2, ROWS // 2, width), BF16),
            pltpu.SemaphoreType.DMA((n_chunks + 11,)),
            pltpu.SemaphoreType.DMA((80,)),
            pltpu.SemaphoreType.DMA((80,)),
        ],
        compiler_params=pltpu.CompilerParams(
            collective_id=0, has_side_effects=True, vmem_limit_bytes=53 << 20
        ),
        name="block",
    )(tokens, gain, w_qkv, gate, w_out)


def settle_kernel(att, state, att_out, state_out):
    att_out[...] = att[...]
    state_out[...] = state[...]


def settle(*arrays):
    vmem = pl.BlockSpec(memory_space=pltpu.VMEM)
    return pl.pallas_call(
        settle_kernel,
        out_shape=tuple(jax.ShapeDtypeStruct(a.shape, a.dtype) for a in arrays),
        in_specs=[vmem, vmem],
        out_specs=(vmem, vmem),
        compiler_params=pltpu.CompilerParams(vmem_limit_bytes=8 << 20),
        name="settle",
    )(*arrays)


def on_device(tokens, norm_gain, w_qkv, mem_gate, w_out):
    norm_gain = pltpu.with_memory_space_constraint(norm_gain, pltpu.HBM)
    mem_gate = pltpu.with_memory_space_constraint(mem_gate, pltpu.HBM)
    return settle(*block(tokens, norm_gain, w_qkv, mem_gate, w_out))


def solution(mesh):
    placed = (P("seq", None), P(), P(None, None, "head"), P("head"), P("head", None))
    return jax.shard_map(
        on_device,
        mesh=mesh,
        in_specs=placed,
        out_specs=(P("seq", "head"), P("seq", "head", None, None)),
        check_vma=False,
    )
```
